32 devices in a mesh: row: 8 (over y, x, core), col: 4 (over z).
Axes of the slice: x: 2, y: 2, z: 4, core: 2. Of those that a mesh axis runs over, the one named last changes fastest.
Arguments:
- matrix: bfloat16 [3072, 3072], P('row', 'col'), may hold values from 3.2484531e-06 to 0.0012969971
- occ_matrix: int32 [24, 24], P('row', 'col'), may hold values 0 or 1
- batch: bfloat16 [3072, 512], P('row', 'col'), may hold values from 0.0099487305 to 4
- occ_batch: int32 [24, 4], P('row', 'col'), may hold values 0 or 1
- prune_mask: int32 [3072, 512], P('row', 'col'), may hold values 0 or 1
Outputs:
- clustered: float32 [3072, 512], P('row', 'col')
The draws below stay inside these ranges and needn't reach their ends.
All inputs are finite; a program needn't handle non-finite values. No bound on the sum of `occ_matrix` or of `occ_batch` or of `prune_mask` on one device may be relied on, other than what follows from the above.
Results may differ from the reference program's by a relative error of at most 0.0003.
Values may be sent and summed in bfloat16 or wider, within the bound.
A program may use at most 64 MiB of HBM per device.

```python
import math
import jax
import jax.numpy as jnp

TILE = 128
N = 3072
NB = 512


def touch_ends(result, own_key, low, high):
    extent = result.shape
    index_at = [jax.random.randint(jax.random.fold_in(own_key, axis), (), 0, extent[axis]) for axis in range(len(extent))]
    result = result.at[tuple(index_at)].set(low)
    longest = extent.index(max(extent))
    index_at[longest] = (index_at[longest] + 1) % extent[longest]
    return result.at[tuple(index_at)].set(high)


def steps_of(key, dims, shards, low, top_value):
    factor_of, own = 1.0, jax.random.fold_in(key, 6)
    for position, shards_of in shards:
        draws = jnp.exp(jax.random.uniform(jax.random.fold_in(own, position), (shards_of,), jnp.float32, low / len(shards), top_value / len(shards)))
        factor_of = factor_of * jnp.repeat(draws, dims[position] // shards_of).reshape([-1 if axis == position else 1 for axis in range(len(dims))])
    return factor_of


def setup_inputs(seed: int = 0) -> dict:
    key_list = jax.random.split(jax.random.key(seed), 6)
    return {
        "matrix": jnp.clip(jnp.exp(math.log(0.0012969971) - 5.989628 * jax.random.uniform(key_list[0], (N, N), jnp.float32) ** steps_of(key_list[0], (N, N), ((0, 8), (1, 4)), -0.2, 0.2)), 3.248453140258789e-06, 0.0012969971).astype(jnp.bfloat16),
        "occ_matrix": touch_ends((jax.random.randint(key_list[1], (N // TILE, N // TILE), 0, 4) < 3).astype(jnp.int32), jax.random.fold_in(key_list[1], 1), 0, 1),
        "batch": jnp.clip(jnp.exp(math.log(4.0) - 5.996605 * jax.random.uniform(key_list[2], (N, NB), jnp.float32) ** steps_of(key_list[2], (N, NB), ((0, 8), (1, 4)), -0.2, 0.2)), 0.0099487305, 4.0).astype(jnp.bfloat16),
        "occ_batch": touch_ends((jax.random.randint(key_list[3], (N // TILE, NB // TILE), 0, 4) < 3).astype(jnp.int32), jax.random.fold_in(key_list[3], 1), 0, 1),
        "prune_mask": touch_ends((jax.random.randint(key_list[4], (N, NB), 0, 8) < 7).astype(jnp.int32), jax.random.fold_in(key_list[4], 1), 0, 1),
    }


def expand_tiles(occupancy, size):
    return jnp.repeat(jnp.repeat(occupancy, size, axis=0), size, axis=1)


def reference(matrix, occ_matrix, batch, occ_batch, prune_mask):
    stored_matrix = matrix * expand_tiles(occ_matrix, TILE).astype(jnp.bfloat16)
    stored_batch = batch * expand_tiles(occ_batch, TILE).astype(jnp.bfloat16)
    expanded = jnp.dot(stored_matrix, stored_batch, preferred_element_type=jnp.float32)
    kept = expanded * prune_mask.astype(jnp.float32)
    inflated = kept * kept
    col_total = jnp.sum(inflated, axis=0)
    return inflated / (col_total[None, :] / N + 1e-5)
```

```python
import functools

import jax
import jax.numpy as jnp
from jax import lax
from jax.experimental import pallas as pl
from jax.experimental.pallas import tpu as pltpu
from jax.sharding import PartitionSpec as P

MESH = pl.DeviceIdType.MESH

LOWEST = -24.0
STEPS = 2047.0
LN2 = 0.6931471805599453


def encode(x):
    safe = jnp.maximum(x, 2.0**LOWEST)
    level = jnp.minimum((jnp.log(safe) * (1.0 / LN2) - LOWEST) * STEPS, 65533.0) + 1.5
    code = jnp.where(x > 0, level.astype(jnp.int32), 0)
    return (code - 32768).astype(jnp.int16)


def decode(code):
    level = code.astype(jnp.int32) + 32767
    value = jnp.exp((level.astype(jnp.float32) * (1.0 / STEPS) + LOWEST) * LN2)
    return jnp.where(level >= 0, value, 0.0)


def expand_tiles(occupancy, size):
    return jnp.repeat(jnp.repeat(occupancy, size, axis=0), size, axis=1)


def plain_body(matrix, occ_matrix, batch, occ_batch, prune_mask):
    tile_size = matrix.shape[0] // occ_matrix.shape[0]
    stored_matrix = matrix * expand_tiles(occ_matrix, tile_size).astype(jnp.bfloat16)
    stored_batch = batch * expand_tiles(occ_batch, tile_size).astype(jnp.bfloat16)
    whole_batch = lax.all_gather(stored_batch, "row", axis=0, tiled=True)
    expanded = jnp.dot(
        lax.all_gather(stored_matrix, "col", axis=1, tiled=True),
        whole_batch,
        preferred_element_type=jnp.float32,
    )
    kept = expanded * prune_mask.astype(jnp.float32)
    inflated = kept * kept
    col_total = lax.psum(jnp.sum(inflated, axis=0), "row")
    order = matrix.shape[0] * lax.axis_size("row")
    return inflated / (col_total[None, :] / order + 1e-05)


def kernel(
    R, C, mat_hbm, occ_m_hbm, bat_hbm, occ_b_hbm, prune_hbm, infl_out, tot_out,
    a_buf, occ_m, bat, occ_b, prune_buf, sb, bk, own, out_buf, in_buf, tots,
    load_sems, s1, r1, s2, r2, f2, zs, zr, ts, tr,
):
    rho = R // C
    rows, depth = a_buf.shape
    piece = rows // C
    tile = rows // occ_m_hbm.shape[0]
    r, c = lax.axis_index("row"), lax.axis_index("col")
    p, e = lax.div(r, rho), lax.rem(r, rho)

    def remote(src, dst, ssem, rsem, row, col):
        return pltpu.make_async_remote_copy(
            src_ref=src, dst_ref=dst, send_sem=ssem, recv_sem=rsem,
            device_id={"row": row, "col": col}, device_id_type=MESH,
        )

    barrier = pltpu.get_barrier_semaphore()

    def greet(row, col):
        pl.semaphore_signal(
            barrier, inc=1, device_id={"row": row, "col": col}, device_id_type=MESH
        )

    for k in range(1, C):
        greet(c * rho + e, lax.rem(c + k, C))
    for k in range(1, R):
        greet(lax.rem(r + k, R), c)

    for k in range(1, C):
        greet(r, lax.rem(c + k, C))

    def load(n, src, dst):
        copy = pltpu.make_async_copy(src, dst, load_sems.at[n])
        copy.start()
        return copy

    load_b = load(0, bat_hbm, bat)
    load_ob = load(1, occ_b_hbm, occ_b)
    load_a = load(2, mat_hbm, a_buf)
    load_om = load(3, occ_m_hbm, occ_m)
    load_prune = load(4, prune_hbm, prune_buf)
    load_ob.wait()
    load_b.wait()
    for t in range(rows // tile):
        part = pl.ds(t * tile, tile)
        sb[part, :] = bat[part, :] * occ_b[t].astype(jnp.float32).astype(jnp.bfloat16)

    greeted = R - 1 + C - 1 + jnp.where(c != p, C, 0)
    pl.semaphore_wait(barrier, greeted)

    def scatter(q):
        return remote(
            sb.at[pl.ds(q * piece, piece)], bk.at[e, q, c],
            s1.at[q], r1.at[c], q * rho + e, p,
        )

    for q in range(C):
        stays = jnp.logical_and(p == q, c == p)

        @pl.when(stays)
        def _():
            pltpu.make_async_copy(
                sb.at[pl.ds(q * piece, piece)], bk.at[e, q, c], r1.at[c]
            ).start()

        @pl.when(jnp.logical_not(stays))
        def _():
            scatter(q).start()

    load_om.wait()
    load_a.wait()
    for i in range(rows // tile):
        for j in range(depth // tile):
            at = (pl.ds(i * tile, tile), pl.ds(j * tile, tile))
            a_buf[at] = a_buf[at] * occ_m[i, j].astype(jnp.float32).astype(jnp.bfloat16)

    sends = []
    reach = jnp.minimum(c, C - 1 - c)

    def nearest(n):
        near = c - (n + 1) // 2 if n % 2 else c + n // 2
        far = jnp.where(c < C - 1 - c, n, C - 1 - n)
        return jnp.where(n <= 2 * reach, near, far)

    order = [nearest(n) for n in list(range(C - 1, 0, -1)) + [0]]

    def send(src, ssem, rsem, row):
        copy = remote(src, src, ssem, rsem, row, c)
        copy.start()
        sends.append(copy)

    def arrived(ref, rsem):
        remote(ref, ref, s1.at[0], rsem, r, c).wait_recv()

    for n, b in enumerate(order):
        mine = bk.at[e, p, b]
        arrived(mine, r1.at[b])
        for k in range(1, C):
            send(mine, s2.at[n, k], r2.at[e, p, b], lax.rem(p + k, C) * rho + e)
        for d in range(1, rho):
            send(mine, f2.at[n, d, 0], r2.at[e, p, b], p * rho + lax.rem(e + d, rho))

    for n, b in enumerate(order):
        for k in range(1, C):
            q = lax.rem(p + k, C)
            got = bk.at[e, q, b]
            arrived(got, r2.at[e, q, b])
            for d in range(1, rho):
                send(got, f2.at[n, d, k], r2.at[e, q, b], p * rho + lax.rem(e + d, rho))
        for d in range(1, rho):
            other = lax.rem(e + d, rho)
            for k in range(C):
                q = lax.rem(p + k, C)
                arrived(bk.at[other, q, b], r2.at[other, q, b])
        rhs = bk[:, :, b].reshape(depth, bk.shape[-1])
        part = jnp.dot(a_buf[...], rhs, preferred_element_type=jnp.float32)
        if n < C - 1:
            out_buf[n] = encode(part)
            copy = remote(out_buf.at[n], in_buf.at[c], zs.at[n], zr.at[c], r, b)
            copy.start()
            sends.append(copy)
        else:
            own[...] = part

    load_prune.wait()
    for n in range(C - 1):
        other = order[C - 2 - n]
        arrived(in_buf.at[other], zr.at[other])
        own[...] = own[...] + decode(in_buf[other])

    kept = own[...] * prune_buf[...].astype(jnp.float32)
    inflated = kept * kept
    tots[r] = jnp.broadcast_to(
        jnp.sum(inflated, axis=0, keepdims=True), tots.shape[1:]
    )
    for k in range(1, R):
        copy = remote(
            tots.at[r], tots.at[r], ts.at[k - 1], tr.at[r], lax.rem(r + k, R), c
        )
        copy.start()
        sends.append(copy)
    for k in range(1, R):
        other = lax.rem(r + k, R)
        got = tots.at[other]
        remote(got, got, ts.at[0], tr.at[other], r, c).wait_recv()
    total = tots[0]
    for k in range(1, R):
        total = total + tots[k]
    infl_out[...] = inflated
    tot_out[...] = total / (rows * R) + 1e-05

    for copy in sends:
        copy.wait_send()
    for q in range(C):
        @pl.when(jnp.logical_not(jnp.logical_and(p == q, c == p)))
        def _():
            scatter(q).wait_send()


def kernel_body(R, C, matrix, occ_matrix, batch, occ_batch, prune_mask):
    rho = R // C
    rows, depth = matrix.shape
    cols = batch.shape[1]
    vmem, hbm = (pl.BlockSpec(memory_space=s) for s in (pltpu.VMEM, pltpu.HBM))
    dma = pltpu.SemaphoreType.DMA
    f32, bf16 = jnp.float32, jnp.bfloat16
    inflated, total = pl.pallas_call(
        functools.partial(kernel, R, C),
        out_shape=(
            pltpu.VMEM((rows, cols), f32),
            pltpu.VMEM((1, cols), f32),
        ),
        in_specs=[hbm] * 5,
        out_specs=(vmem, vmem),
        scratch_shapes=[
            pltpu.VMEM((rows, depth), bf16),
            pltpu.SMEM(occ_matrix.shape, jnp.int32),
            pltpu.VMEM((rows, cols), bf16),
            pltpu.SMEM(occ_batch.shape[:1], jnp.int32),
            pltpu.VMEM((rows, cols), jnp.int32),
            pltpu.VMEM((rows, cols), bf16),
            pltpu.VMEM((rho, C, C, rows // C, cols), bf16),
            pltpu.VMEM((rows, cols), f32),
            pltpu.VMEM((C - 1, rows, cols), jnp.int16),
            pltpu.VMEM((C, rows, cols), jnp.int16),
            pltpu.VMEM((R, 1, cols), f32),
            dma((5,)),
            dma((C,)),
            dma((C,)),
            dma((C, C)),
            dma((rho, C, C)),
            dma((C, rho, C)),
            dma((C - 1,)),
            dma((C,)),
            dma((R - 1,)),
            dma((R,)),
        ],
        compiler_params=pltpu.CompilerParams(
            collective_id=0, has_side_effects=True, vmem_limit_bytes=32 * 2**20
        ),
    )(*(
        pltpu.with_memory_space_constraint(x, pltpu.HBM)
        for x in (matrix, occ_matrix, batch, occ_batch[:, 0], prune_mask)
    ))
    return inflated / total


def body(R, C, matrix, occ_matrix, batch, occ_batch, prune_mask):
    rows = matrix.shape[0]
    fits = (
        1 < C <= 8 and R % C == 0 and R <= 16
        and rows % (16 * C) == 0 and matrix.shape[1] == rows * (R // C)
    )
    chosen = functools.partial(kernel_body, R, C) if fits else plain_body
    return chosen(matrix, occ_matrix, batch, occ_batch, prune_mask)


def solution(mesh):
    R, C = mesh.shape["row"], mesh.shape["col"]
    placed = (P("row", "col"),) * 5
    return jax.shard_map(
        functools.partial(body, R, C), mesh=mesh, in_specs=placed,
        out_specs=P("row", "col"), check_vma=False,
    )
```

```python
import functools

import jax
import jax.numpy as jnp
from jax import lax
from jax.experimental import pallas as pl
from jax.experimental.pallas import tpu as pltpu
from jax.sharding import PartitionSpec as P

MESH = pl.DeviceIdType.MESH

LOWEST = -20.5
STEPS = 2730.0
LN2 = 0.6931471805599453


def encode(x):
    safe = jnp.maximum(x, 2.0**LOWEST)
    level = jnp.minimum((jnp.log(safe) * (1.0 / LN2) - LOWEST) * STEPS, 65533.0) + 1.5
    code = jnp.where(x > 0, level.astype(jnp.int32), 0)
    return (code - 32768).astype(jnp.int16)


def decode(code):
    level = code.astype(jnp.int32) + 32767
    value = jnp.exp((level.astype(jnp.float32) * (1.0 / STEPS) + LOWEST) * LN2)
    return jnp.where(level >= 0, value, 0.0)


def expand_tiles(occupancy, size):
    return jnp.repeat(jnp.repeat(occupancy, size, axis=0), size, axis=1)


def plain_body(matrix, occ_matrix, batch, occ_batch, prune_mask):
    tile_size = matrix.shape[0] // occ_matrix.shape[0]
    stored_matrix = matrix * expand_tiles(occ_matrix, tile_size).astype(jnp.bfloat16)
    stored_batch = batch * expand_tiles(occ_batch, tile_size).astype(jnp.bfloat16)
    whole_batch = lax.all_gather(stored_batch, "row", axis=0, tiled=True)
    expanded = jnp.dot(
        lax.all_gather(stored_matrix, "col", axis=1, tiled=True),
        whole_batch,
        preferred_element_type=jnp.float32,
    )
    kept = expanded * prune_mask.astype(jnp.float32)
    inflated = kept * kept
    col_total = lax.psum(jnp.sum(inflated, axis=0), "row")
    order = matrix.shape[0] * lax.axis_size("row")
    return inflated / (col_total[None, :] / order + 1e-05)


def kernel(
    R, C, mat_hbm, occ_m_hbm, bat_hbm, occ_b_hbm, prune_hbm, infl_out, tot_out,
    both, occ_m, bat, occ_b, prune_buf, sb, bk, part, near, out_buf, in_buf, tots,
    load_sems, swap_s, swap_r, s1, r1, s2, r2, zs, zr, near_s, near_r, ts, tr,
):
    half = C // 2
    _, rows, depth = both.shape
    piece = rows // C
    tile = rows // occ_m_hbm.shape[0]
    r, c = lax.axis_index("row"), lax.axis_index("col")
    p, e = lax.div(r, 2), lax.rem(r, 2)
    other = 1 - e
    keeper, slot = 1 - lax.div(c, half), lax.rem(c, half)
    mine_half = 1 - e

    def flip(at, k):
        for bit in (1, 2, 4):
            if k & bit:
                at = at + bit * (1 - 2 * lax.rem(lax.div(at, bit), 2))
        return at

    def remote(src, dst, ssem, rsem, chip, core, plane):
        return pltpu.make_async_remote_copy(
            src_ref=src, dst_ref=dst, send_sem=ssem, recv_sem=rsem,
            device_id={"row": chip * 2 + core, "col": plane}, device_id_type=MESH,
        )

    def arrived(ref, rsem):
        remote(ref, ref, s1.at[0], rsem, p, e, c).wait_recv()

    def signal(sem, chip, core, plane):
        pl.semaphore_signal(
            sem, inc=1, device_id={"row": chip * 2 + core, "col": plane},
            device_id_type=MESH,
        )

    barrier = pltpu.get_barrier_semaphore()

    for k in range(1, R):
        there = lax.rem(r + k, R)
        signal(barrier, lax.div(there, 2), lax.rem(there, 2), c)
    for n in range(half):
        b = mine_half * half + n
        for core in range(2):
            @pl.when(b != c)
            def _():
                signal(barrier, c, core, b)
    for k in range(1, C):
        signal(barrier, p, keeper, lax.rem(c + k, C))

    def load(n, src, dst):
        copy = pltpu.make_async_copy(src, dst, load_sems.at[n])
        copy.start()
        return copy

    load_b = load(0, bat_hbm, bat)
    load_ob = load(1, occ_b_hbm, occ_b)
    load_a = load(2, mat_hbm, both.at[e])
    load_om = load(3, occ_m_hbm, occ_m)
    load_prune = load(4, prune_hbm, prune_buf)
    load_ob.wait()
    load_b.wait()
    for t in range(rows // tile):
        at = pl.ds(t * tile, tile)
        sb[at, :] = bat[at, :] * occ_b[t].astype(jnp.float32).astype(jnp.bfloat16)

    with jax.named_scope("greeted"):
        pl.semaphore_wait(barrier, R - 1 + jnp.where(p != c, C, 0) + C - jnp.where(keeper == e, 2, 0))

    def scatter(q):
        return remote(
            sb.at[pl.ds(q * piece, piece)], bk.at[slot, e, q],
            s1.at[q], r1.at[slot, e], q, keeper, p,
        )

    def stays(q):
        return jnp.logical_and(jnp.logical_and(p == q, c == p), keeper == e)

    def spread():
        for k in range(C - 1, -1, -1):
            q = flip(p, k)

            @pl.when(stays(q))
            def _():
                pltpu.make_async_copy(
                    sb.at[pl.ds(q * piece, piece)], bk.at[slot, e, q], r1.at[slot, e]
                ).start()

            @pl.when(jnp.logical_not(stays(q)))
            def _():
                scatter(q).start()

    crosses = lax.div(p, half) != lax.div(c, half)
    spread()

    load_om.wait()
    load_a.wait()
    for i in range(rows // tile):
        for j in range(depth // tile):
            at = (e, pl.ds(i * tile, tile), pl.ds(j * tile, tile))
            both[at] = both[at] * occ_m[i, j].astype(jnp.float32).astype(jnp.bfloat16)
    sends = []

    def send(*args):
        copy = remote(*args)
        copy.start()
        sends.append(copy)

    send(both.at[e], both.at[e], swap_s.at[0], swap_r.at[0], p, other, c)

    first = jnp.where(keeper == e, 1 - slot, mine_half)
    order = [first, 1 - first]

    def pass_on(n, at):
        for core in range(2):
            mine = bk.at[at, core, p]
            with jax.named_scope("piece"):
                arrived(mine, r1.at[at, core])
            for k in range(C - 1, 0, -1):
                send(mine, mine, s2.at[n, core, k], r2.at[at, core, p], flip(p, k), e, c)

    def gather(at):
        with jax.named_scope("block"):
            for core in range(2):
                for k in range(1, C):
                    q = flip(p, k)
                    arrived(bk.at[at, core, q], r2.at[at, core, q])
        return bk[at].reshape(depth, bk.shape[-1])

    def product(core, rhs):
        return jnp.dot(both[core], rhs, preferred_element_type=jnp.float32)

    def partial_out(n, core, b):
        return remote(out_buf.at[n, core], in_buf.at[c], zs.at[n, core], zr.at[c], p, core, b)

    def to_near():
        return remote(part.at[other], near.at[0], near_s.at[0], near_r.at[0], p, other, c)

    across, beside = mine_half * half + order[0], mine_half * half + order[1]
    pass_on(0, order[0])
    with jax.named_scope("swap"):
        arrived(both.at[other], swap_r.at[0])
    rhs = gather(order[0])
    for core in range(2):
        part[core] = product(core, rhs)

        out_buf[0, core] = encode(part[core])

        partial_out(0, core, across).start()

    pass_on(1, order[1])
    rhs = gather(order[1])
    for core in range(2):
        part[core] = product(core, rhs)

        @pl.when(beside != c)
        def _():
            out_buf[1, core] = encode(part[core])
            partial_out(1, core, beside).start()

    @pl.when(beside == c)
    def _():
        to_near().start()

    @pl.when(keeper != e)
    def _():
        with jax.named_scope("near"):
            arrived(near.at[0], near_r.at[0])

    @pl.when(keeper == e)
    def _():
        near[0] = part[e]

    load_prune.wait()
    for k in range(1, C):
        s = flip(c, k)

        def take():
            with jax.named_scope("partial"):
                arrived(in_buf.at[s], zr.at[s])
            near[0] = near[0] + decode(in_buf[s])

        take()

    own = near[0]
    kept = own * prune_buf[...].astype(jnp.float32)
    inflated = kept * kept
    infl_out[...] = inflated
    tots[r] = jnp.broadcast_to(
        jnp.sum(inflated, axis=0, keepdims=True), tots.shape[1:]
    )
    for k in range(1, R):
        there = flip(r, R - k)
        send(tots.at[r], tots.at[r], ts.at[k - 1], tr.at[r], lax.div(there, 2), lax.rem(there, 2), c)
    with jax.named_scope("totals"):
        for k in range(1, R):
            there = lax.rem(r + k, R)
            arrived(tots.at[there], tr.at[there])
    total = tots[0]
    for k in range(1, R):
        total = total + tots[k]
    tot_out[...] = total / (rows * R) + 1e-05

    with jax.named_scope("sent"):
        for copy in sends:
            copy.wait_send()
        for q in range(C):
            @pl.when(jnp.logical_not(stays(q)))
            def _():
                scatter(q).wait_send()
        for core in range(2):
            partial_out(0, core, across).wait_send()

            @pl.when(beside != c)
            def _():
                partial_out(1, core, beside).wait_send()

        @pl.when(beside == c)
        def _():
            to_near().wait_send()


def kernel_body(R, C, matrix, occ_matrix, batch, occ_batch, prune_mask):
    rows, depth = matrix.shape
    cols = batch.shape[1]
    half = C // 2
    vmem, hbm = (pl.BlockSpec(memory_space=s) for s in (pltpu.VMEM, pltpu.HBM))
    dma = pltpu.SemaphoreType.DMA
    f32, bf16 = jnp.float32, jnp.bfloat16
    inflated, total = pl.pallas_call(
        functools.partial(kernel, R, C),
        out_shape=(
            pltpu.VMEM((rows, cols), f32),
            pltpu.VMEM((1, cols), f32),
        ),
        in_specs=[hbm] * 5,
        out_specs=(vmem, vmem),
        scratch_shapes=[
            pltpu.VMEM((2, rows, depth), bf16),
            pltpu.SMEM(occ_matrix.shape, jnp.int32),
            pltpu.VMEM((rows, cols), bf16),
            pltpu.SMEM(occ_batch.shape[:1], jnp.int32),
            pltpu.VMEM((rows, cols), jnp.int32),
            pltpu.VMEM((rows, cols), bf16),
            pltpu.VMEM((half, 2, C, rows // C, cols), bf16),
            pltpu.VMEM((2, rows, cols), f32),
            pltpu.VMEM((1, rows, cols), f32),
            pltpu.VMEM((half, 2, rows, cols), jnp.int16),
            pltpu.VMEM((C, rows, cols), jnp.int16),
            pltpu.VMEM((R, 1, cols), f32),
            dma((5,)),
            dma((1,)),
            dma((1,)),
            dma((C,)),
            dma((half, 2)),
            dma((half, 2, C)),
            dma((half, 2, C)),
            dma((half, 2)),
            dma((C,)),
            dma((1,)),
            dma((1,)),
            dma((R - 1,)),
            dma((R,)),
        ],
        compiler_params=pltpu.CompilerParams(
            collective_id=0, has_side_effects=True, vmem_limit_bytes=32 * 2**20
        ),
    )(*(
        pltpu.with_memory_space_constraint(x, pltpu.HBM)
        for x in (matrix, occ_matrix, batch, occ_batch[:, 0], prune_mask)
    ))
    return inflated / total


def body(R, C, matrix, occ_matrix, batch, occ_batch, prune_mask):
    rows = matrix.shape[0]
    fits = (
        C == 4 and R == 2 * C
        and rows % (16 * C) == 0 and matrix.shape[1] == rows * 2
    )
    chosen = functools.partial(kernel_body, R, C) if fits else plain_body
    return chosen(matrix, occ_matrix, batch, occ_batch, prune_mask)


def solution(mesh):
    R, C = mesh.shape["row"], mesh.shape["col"]
    placed = (P("row", "col"),) * 5
    return jax.shard_map(
        functools.partial(body, R, C), mesh=mesh, in_specs=placed,
        out_specs=P("row", "col"), check_vma=False,
    )
```

```python
import functools

import jax
import jax.numpy as jnp
from jax import lax
from jax.experimental import pallas as pl
from jax.experimental.pallas import tpu as pltpu
from jax.sharding import PartitionSpec as P

MESH = pl.DeviceIdType.MESH

LOWEST = -20.5
STEPS = 2730.0
HOPS = (1,)
LN2 = 0.6931471805599453


def encode(x):
    safe = jnp.maximum(x, 2.0**LOWEST)
    level = jnp.minimum((jnp.log(safe) * (1.0 / LN2) - LOWEST) * STEPS, 65533.0) + 1.5
    code = jnp.where(x > 0, level.astype(jnp.int32), 0)
    return (code - 32768).astype(jnp.int16)


def decode(code):
    level = code.astype(jnp.int32) + 32767
    value = jnp.exp((level.astype(jnp.float32) * (1.0 / STEPS) + LOWEST) * LN2)
    return jnp.where(level >= 0, value, 0.0)


def expand_tiles(occupancy, size):
    return jnp.repeat(jnp.repeat(occupancy, size, axis=0), size, axis=1)


def plain_body(matrix, occ_matrix, batch, occ_batch, prune_mask):
    tile_size = matrix.shape[0] // occ_matrix.shape[0]
    stored_matrix = matrix * expand_tiles(occ_matrix, tile_size).astype(jnp.bfloat16)
    stored_batch = batch * expand_tiles(occ_batch, tile_size).astype(jnp.bfloat16)
    whole_batch = lax.all_gather(stored_batch, "row", axis=0, tiled=True)
    expanded = jnp.dot(
        lax.all_gather(stored_matrix, "col", axis=1, tiled=True),
        whole_batch,
        preferred_element_type=jnp.float32,
    )
    kept = expanded * prune_mask.astype(jnp.float32)
    inflated = kept * kept
    col_total = lax.psum(jnp.sum(inflated, axis=0), "row")
    order = matrix.shape[0] * lax.axis_size("row")
    return inflated / (col_total[None, :] / order + 1e-05)


def kernel(
    R, C, mat_hbm, occ_m_hbm, bat_hbm, occ_b_hbm, prune_hbm, infl_out, tot_out,
    both, occ_m, bat, occ_b, prune_buf, sb, bk, part, near, out_buf, in_buf, hop, tots,
    load_sems, swap_s, swap_r, s1, r1, s2, r2, zs, zr, near_s, near_r, ts, tr,
    hop_s, hop_r, ready, ready_row,
):
    half = C // 2
    _, rows, depth = both.shape
    piece = rows // C
    tile = rows // occ_m_hbm.shape[0]
    r, c = lax.axis_index("row"), lax.axis_index("col")
    p, e = lax.div(r, 2), lax.rem(r, 2)
    other = 1 - e
    keeper, slot = 1 - lax.div(c, half), lax.rem(c, half)
    mine_half = 1 - e

    def flip(at, k):
        for bit in (1, 2, 4):
            if k & bit:
                at = at + bit * (1 - 2 * lax.rem(lax.div(at, bit), 2))
        return at

    def remote(src, dst, ssem, rsem, chip, core, plane):
        return pltpu.make_async_remote_copy(
            src_ref=src, dst_ref=dst, send_sem=ssem, recv_sem=rsem,
            device_id={"row": chip * 2 + core, "col": plane}, device_id_type=MESH,
        )

    def arrived(ref, rsem):
        remote(ref, ref, s1.at[0], rsem, p, e, c).wait_recv()

    def signal(sem, chip, core, plane):
        pl.semaphore_signal(
            sem, inc=1, device_id={"row": chip * 2 + core, "col": plane},
            device_id_type=MESH,
        )

    barrier = pltpu.get_barrier_semaphore()

    def guarded(condition, *args):
        @pl.when(condition)
        def _():
            signal(*args)

    for n in range(half):
        b = mine_half * half + n
        for core in range(2):
            guarded(b != c, barrier, c, core, b)
    crossing = keeper != e
    lends = jnp.logical_and(crossing, c == 0)
    joins = jnp.logical_and(crossing, c == 1)
    guarded(joins, barrier, p, e, 0)
    for k in range(R):
        guarded(k > r, barrier, k // 2, k % 2, c)
    for n in range(half):
        b = mine_half * half + n
        for core in range(2):
            guarded(b > c, barrier, p, core, b)
    for s in range(1, C):
        guarded(s > c, barrier, p, keeper, s)

    def load(n, src, dst):
        copy = pltpu.make_async_copy(src, dst, load_sems.at[n])
        copy.start()
        return copy

    load_b = load(0, bat_hbm, bat)
    load_ob = load(1, occ_b_hbm, occ_b)
    load_a = load(2, mat_hbm, both.at[e])
    load_om = load(3, occ_m_hbm, occ_m)
    load_prune = load(4, prune_hbm, prune_buf)
    load_ob.wait()
    load_b.wait()
    for t in range(rows // tile):
        at = pl.ds(t * tile, tile)
        sb[at, :] = bat[at, :] * occ_b[t].astype(jnp.float32).astype(jnp.bfloat16)

    earlier = r + c + jnp.where(p != c, C, 0) + jnp.where(lends, 1, 0)
    for n in range(half):
        earlier = earlier + jnp.where(mine_half * half + n < c, 2, 0)
    with jax.named_scope("greeted"):
        pl.semaphore_wait(barrier, earlier)

    def scatter(q):
        return remote(
            sb.at[pl.ds(q * piece, piece)], bk.at[slot, e, q],
            s1.at[q], r1.at[slot, e], q, keeper, p,
        )

    def stays(q):
        return jnp.logical_and(jnp.logical_and(p == q, c == p), keeper == e)

    def spread():
        for k in range(C - 1, -1, -1):
            q = flip(p, k)

            @pl.when(stays(q))
            def _():
                pltpu.make_async_copy(
                    sb.at[pl.ds(q * piece, piece)], bk.at[slot, e, q], r1.at[slot, e]
                ).start()

            @pl.when(jnp.logical_not(stays(q)))
            def _():
                scatter(q).start()

    crosses = lax.div(p, half) != lax.div(c, half)
    pl.when(p != c)(spread)
    for k in range(R):
        guarded(k < r, ready_row.at[0], k // 2, k % 2, c)
    for s in range(C - 1):
        guarded(s < c, ready.at[slot, e], p, keeper, s)

    load_om.wait()
    load_a.wait()
    for i in range(rows // tile):
        for j in range(depth // tile):
            at = (e, pl.ds(i * tile, tile), pl.ds(j * tile, tile))
            both[at] = both[at] * occ_m[i, j].astype(jnp.float32).astype(jnp.bfloat16)

    @pl.when(r < R - 1)
    def _():
        with jax.named_scope("row"):
            pl.semaphore_wait(ready_row.at[0], R - 1 - r)

    sends = []

    def send(*args):
        copy = remote(*args)
        copy.start()
        sends.append(copy)

    send(both.at[e], both.at[e], swap_s.at[0], swap_r.at[0], p, other, c)
    pl.when(p == c)(spread)

    first = jnp.where(keeper == e, 1 - slot, jnp.where(c == 1, 0, mine_half))
    order = [first, 1 - first]

    def pass_on(n, at):
        for core in range(2):
            mine = bk.at[at, core, p]
            with jax.named_scope("piece"):
                arrived(mine, r1.at[at, core])
            for k in range(C - 1, 0, -1):
                send(mine, mine, s2.at[n, core, k], r2.at[at, core, p], flip(p, k), e, c)

    def gather(at):
        with jax.named_scope("block"):
            for core in range(2):
                for k in range(1, C):
                    q = flip(p, k)
                    arrived(bk.at[at, core, q], r2.at[at, core, q])
        return bk[at].reshape(depth, bk.shape[-1])

    def product(core, rhs):
        return jnp.dot(both[core], rhs, preferred_element_type=jnp.float32)

    def partial_out(n, core, b):
        return remote(out_buf.at[n, core], in_buf.at[c], zs.at[n, core], zr.at[c], p, core, b)

    def to_hop(core):
        return remote(out_buf.at[0, core], hop.at[core], hop_s.at[core], hop_r.at[core], p, e, 1)

    def to_near():
        return remote(part.at[other], near.at[0], near_s.at[0], near_r.at[0], p, other, c)

    across, beside = mine_half * half + order[0], mine_half * half + order[1]
    pass_on(0, order[0])
    with jax.named_scope("swap"):
        arrived(both.at[other], swap_r.at[0])
    pass_on(1, order[1])
    rhs = gather(order[0])
    for at in order:
        for core in range(2):
            @pl.when(mine_half * half + at > c)
            def _():
                pl.semaphore_wait(ready.at[at, core], 1)
    for core in range(2):
        part[core] = product(core, rhs)

        out_buf[0, core] = encode(part[core])


        by_hop = lends if core in HOPS else c < 0

        @pl.when(by_hop)
        def _():
            to_hop(core).start()

        @pl.when(jnp.logical_not(by_hop))
        def _():
            partial_out(0, core, across).start()

    rhs = gather(order[1])
    for core in range(2):
        part[core] = product(core, rhs)

        @pl.when(joins if core in HOPS else c < 0)
        def _():
            with jax.named_scope("hop"):
                arrived(hop.at[core], hop_r.at[core])
            part[core] = part[core] + decode(hop[core])

        @pl.when(beside != c)
        def _():
            out_buf[1, core] = encode(part[core])
            partial_out(1, core, beside).start()

    @pl.when(beside == c)
    def _():
        to_near().start()

    @pl.when(keeper != e)
    def _():
        with jax.named_scope("near"):
            arrived(near.at[0], near_r.at[0])

    @pl.when(keeper == e)
    def _():
        near[0] = part[e]

    load_prune.wait()
    for k in range(1, C):
        s = flip(c, k)

        def take():
            with jax.named_scope("partial"):
                arrived(in_buf.at[s], zr.at[s])
            near[0] = near[0] + decode(in_buf[s])

        if k == C - 1:
            pl.when(jnp.logical_or(c != C - 1, e != HOPS[0]))(take)
        else:
            take()

    own = near[0]
    kept = own * prune_buf[...].astype(jnp.float32)
    inflated = kept * kept
    infl_out[...] = inflated
    tots[r] = jnp.broadcast_to(
        jnp.sum(inflated, axis=0, keepdims=True), tots.shape[1:]
    )
    for k in range(1, R):
        there = flip(r, R - k)
        send(tots.at[r], tots.at[r], ts.at[k - 1], tr.at[r], lax.div(there, 2), lax.rem(there, 2), c)
    with jax.named_scope("totals"):
        for k in range(1, R):
            there = lax.rem(r + k, R)
            arrived(tots.at[there], tr.at[there])
    total = tots[0]
    for k in range(1, R):
        total = total + tots[k]
    tot_out[...] = total / (rows * R) + 1e-05

    with jax.named_scope("sent"):
        for copy in sends:
            copy.wait_send()
        for q in range(C):
            @pl.when(jnp.logical_not(stays(q)))
            def _():
                scatter(q).wait_send()
        for core in range(2):
            by_hop = lends if core in HOPS else c < 0

            @pl.when(by_hop)
            def _():
                to_hop(core).wait_send()

            @pl.when(jnp.logical_not(by_hop))
            def _():
                partial_out(0, core, across).wait_send()

            @pl.when(beside != c)
            def _():
                partial_out(1, core, beside).wait_send()

        @pl.when(beside == c)
        def _():
            to_near().wait_send()


def kernel_body(R, C, matrix, occ_matrix, batch, occ_batch, prune_mask):
    rows, depth = matrix.shape
    cols = batch.shape[1]
    half = C // 2
    vmem, hbm = (pl.BlockSpec(memory_space=s) for s in (pltpu.VMEM, pltpu.HBM))
    dma = pltpu.SemaphoreType.DMA
    f32, bf16 = jnp.float32, jnp.bfloat16
    inflated, total = pl.pallas_call(
        functools.partial(kernel, R, C),
        out_shape=(
            pltpu.VMEM((rows, cols), f32),
            pltpu.VMEM((1, cols), f32),
        ),
        in_specs=[hbm] * 5,
        out_specs=(vmem, vmem),
        scratch_shapes=[
            pltpu.VMEM((2, rows, depth), bf16),
            pltpu.SMEM(occ_matrix.shape, jnp.int32),
            pltpu.VMEM((rows, cols), bf16),
            pltpu.SMEM(occ_batch.shape[:1], jnp.int32),
            pltpu.VMEM((rows, cols), jnp.int32),
            pltpu.VMEM((rows, cols), bf16),
            pltpu.VMEM((half, 2, C, rows // C, cols), bf16),
            pltpu.VMEM((2, rows, cols), f32),
            pltpu.VMEM((1, rows, cols), f32),
            pltpu.VMEM((half, 2, rows, cols), jnp.int16),
            pltpu.VMEM((C, rows, cols), jnp.int16),
            pltpu.VMEM((2, rows, cols), jnp.int16),
            pltpu.VMEM((R, 1, cols), f32),
            dma((5,)),
            dma((1,)),
            dma((1,)),
            dma((C,)),
            dma((half, 2)),
            dma((half, 2, C)),
            dma((half, 2, C)),
            dma((half, 2)),
            dma((C,)),
            dma((1,)),
            dma((1,)),
            dma((R - 1,)),
            dma((R,)),
            dma((2,)),
            dma((2,)),
            pltpu.SemaphoreType.REGULAR((half, 2)),
            pltpu.SemaphoreType.REGULAR((1,)),
        ],
        compiler_params=pltpu.CompilerParams(
            collective_id=0, has_side_effects=True, vmem_limit_bytes=32 * 2**20
        ),
    )(*(
        pltpu.with_memory_space_constraint(x, pltpu.HBM)
        for x in (matrix, occ_matrix, batch, occ_batch[:, 0], prune_mask)
    ))
    return inflated / total


def body(R, C, matrix, occ_matrix, batch, occ_batch, prune_mask):
    rows = matrix.shape[0]
    fits = (
        C == 4 and R == 2 * C
        and rows % (16 * C) == 0 and matrix.shape[1] == rows * 2
    )
    chosen = functools.partial(kernel_body, R, C) if fits else plain_body
    return chosen(matrix, occ_matrix, batch, occ_batch, prune_mask)


def solution(mesh):
    R, C = mesh.shape["row"], mesh.shape["col"]
    placed = (P("row", "col"),) * 5
    return jax.shard_map(
        functools.partial(body, R, C), mesh=mesh, in_specs=placed,
        out_specs=P("row", "col"), check_vma=False,
    )
```

```python
import functools

import jax
import jax.numpy as jnp
from jax import lax
from jax.experimental import pallas as pl
from jax.experimental.pallas import tpu as pltpu
from jax.sharding import PartitionSpec as P

MESH = pl.DeviceIdType.MESH

LOWEST = -20.5
STEPS = 2730.0
HOPS = (1,)
LN2 = 0.6931471805599453


def encode(x):
    safe = jnp.maximum(x, 2.0**LOWEST)
    level = jnp.minimum((jnp.log(safe) * (1.0 / LN2) - LOWEST) * STEPS, 65533.0) + 1.5
    code = jnp.where(x > 0, level.astype(jnp.int32), 0)
    return (code - 32768).astype(jnp.int16)


def decode(code):
    level = code.astype(jnp.int32) + 32767
    value = jnp.exp((level.astype(jnp.float32) * (1.0 / STEPS) + LOWEST) * LN2)
    return jnp.where(level >= 0, value, 0.0)


def expand_tiles(occupancy, size):
    return jnp.repeat(jnp.repeat(occupancy, size, axis=0), size, axis=1)


def plain_body(matrix, occ_matrix, batch, occ_batch, prune_mask):
    tile_size = matrix.shape[0] // occ_matrix.shape[0]
    stored_matrix = matrix * expand_tiles(occ_matrix, tile_size).astype(jnp.bfloat16)
    stored_batch = batch * expand_tiles(occ_batch, tile_size).astype(jnp.bfloat16)
    whole_batch = lax.all_gather(stored_batch, "row", axis=0, tiled=True)
    expanded = jnp.dot(
        lax.all_gather(stored_matrix, "col", axis=1, tiled=True),
        whole_batch,
        preferred_element_type=jnp.float32,
    )
    kept = expanded * prune_mask.astype(jnp.float32)
    inflated = kept * kept
    col_total = lax.psum(jnp.sum(inflated, axis=0), "row")
    order = matrix.shape[0] * lax.axis_size("row")
    return inflated / (col_total[None, :] / order + 1e-05)


def kernel(
    R, C, mat_hbm, occ_m_hbm, bat_hbm, occ_b_hbm, prune_hbm, infl_out, tot_out,
    both, occ_m, bat, occ_b, prune_buf, sb, bk, part, near, out_buf, in_buf, hop, tots,
    load_sems, swap_s, swap_r, s1, r1, s2, r2, zs, zr, near_s, near_r, ts, tr,
    hop_s, hop_r, ready, ready_row,
):
    half = C // 2
    _, rows, depth = both.shape
    piece = rows // C
    tile = rows // occ_m_hbm.shape[0]
    r, c = lax.axis_index("row"), lax.axis_index("col")
    p, e = lax.div(r, 2), lax.rem(r, 2)
    other = 1 - e
    keeper, slot = 1 - lax.div(c, half), lax.rem(c, half)
    mine_half = 1 - e

    def flip(at, k):
        for bit in (1, 2, 4):
            if k & bit:
                at = at + bit * (1 - 2 * lax.rem(lax.div(at, bit), 2))
        return at

    def remote(src, dst, ssem, rsem, chip, core, plane):
        return pltpu.make_async_remote_copy(
            src_ref=src, dst_ref=dst, send_sem=ssem, recv_sem=rsem,
            device_id={"row": chip * 2 + core, "col": plane}, device_id_type=MESH,
        )

    def arrived(ref, rsem):
        remote(ref, ref, s1.at[0], rsem, p, e, c).wait_recv()

    def signal(sem, chip, core, plane):
        pl.semaphore_signal(
            sem, inc=1, device_id={"row": chip * 2 + core, "col": plane},
            device_id_type=MESH,
        )

    barrier = pltpu.get_barrier_semaphore()

    def guarded(condition, *args):
        @pl.when(condition)
        def _():
            signal(*args)

    for n in range(half):
        b = mine_half * half + n
        for core in range(2):
            guarded(b != c, barrier, c, core, b)
    crossing = keeper != e
    lends = jnp.logical_and(crossing, c == 0)
    joins = jnp.logical_and(crossing, c == 1)
    guarded(joins, barrier, p, e, 0)
    for k in range(R):
        guarded(k > r, barrier, k // 2, k % 2, c)
    for n in range(half):
        b = mine_half * half + n
        for core in range(2):
            guarded(b > c, barrier, p, core, b)
    for s in range(1, C):
        guarded(s > c, barrier, p, keeper, s)

    def load(n, src, dst):
        copy = pltpu.make_async_copy(src, dst, load_sems.at[n])
        copy.start()
        return copy

    load_b = load(0, bat_hbm, bat)
    load_ob = load(1, occ_b_hbm, occ_b)
    load_a = load(2, mat_hbm, both.at[e])
    load_om = load(3, occ_m_hbm, occ_m)
    load_prune = load(4, prune_hbm, prune_buf)
    load_ob.wait()
    load_b.wait()
    for t in range(rows // tile):
        at = pl.ds(t * tile, tile)
        sb[at, :] = bat[at, :] * occ_b[t].astype(jnp.float32).astype(jnp.bfloat16)

    earlier = r + c + jnp.where(p != c, C, 0) + jnp.where(lends, 1, 0)
    for n in range(half):
        earlier = earlier + jnp.where(mine_half * half + n < c, 2, 0)
    with jax.named_scope("greeted"):
        pl.semaphore_wait(barrier, earlier)

    def scatter(q):
        return remote(
            sb.at[pl.ds(q * piece, piece)], bk.at[slot, e, q],
            s1.at[q], r1.at[slot, e], q, keeper, p,
        )

    def stays(q):
        return jnp.logical_and(jnp.logical_and(p == q, c == p), keeper == e)

    def spread():
        for k in range(C - 1, -1, -1):
            q = flip(p, k)

            @pl.when(stays(q))
            def _():
                pltpu.make_async_copy(
                    sb.at[pl.ds(q * piece, piece)], bk.at[slot, e, q], r1.at[slot, e]
                ).start()

            @pl.when(jnp.logical_not(stays(q)))
            def _():
                scatter(q).start()

    crosses = lax.div(p, half) != lax.div(c, half)
    pl.when(p != c)(spread)
    for k in range(R):
        guarded(k < r, ready_row.at[0], k // 2, k % 2, c)
    for s in range(C - 1):
        guarded(s < c, ready.at[slot, e], p, keeper, s)

    load_om.wait()
    load_a.wait()
    for i in range(rows // tile):
        for j in range(depth // tile):
            at = (e, pl.ds(i * tile, tile), pl.ds(j * tile, tile))
            both[at] = both[at] * occ_m[i, j].astype(jnp.float32).astype(jnp.bfloat16)

    @pl.when(r < R - 1)
    def _():
        with jax.named_scope("row"):
            pl.semaphore_wait(ready_row.at[0], R - 1 - r)

    sends = []

    def send(*args):
        copy = remote(*args)
        copy.start()
        sends.append(copy)

    send(both.at[e], both.at[e], swap_s.at[0], swap_r.at[0], p, other, c)
    pl.when(p == c)(spread)

    first = jnp.where(keeper == e, 1 - slot, jnp.where(c == 1, 0, mine_half))
    order = [first, 1 - first]

    def pass_on(n, at):
        for core in range(2):
            mine = bk.at[at, core, p]
            with jax.named_scope("piece"):
                arrived(mine, r1.at[at, core])
            for k in range(C - 1, 0, -1):
                remote(mine, mine, s2.at[0], r2.at[at], flip(p, k), e, c).start()

    def gather(at):
        with jax.named_scope("block"):
            arrived(bk.at[at, :, pl.ds(0, C - 1)], r2.at[at])
        return bk[at].reshape(depth, bk.shape[-1])

    def product(core, rhs):
        return jnp.dot(both[core], rhs, preferred_element_type=jnp.float32)

    def partial_out(n, core, b):
        return remote(out_buf.at[n, core], in_buf.at[c], zs.at[n, core], zr.at[c], p, core, b)

    def to_hop(core):
        return remote(out_buf.at[0, core], hop.at[core], hop_s.at[core], hop_r.at[core], p, e, 1)

    def to_near():
        return remote(part.at[other], near.at[0], near_s.at[0], near_r.at[0], p, other, c)

    across, beside = mine_half * half + order[0], mine_half * half + order[1]
    pass_on(0, order[0])
    with jax.named_scope("swap"):
        arrived(both.at[other], swap_r.at[0])
    pass_on(1, order[1])
    rhs = gather(order[0])
    for at in order:
        for core in range(2):
            @pl.when(mine_half * half + at > c)
            def _():
                pl.semaphore_wait(ready.at[at, core], 1)
    for core in range(2):
        part[core] = product(core, rhs)

        out_buf[0, core] = encode(part[core])


        by_hop = lends if core in HOPS else c < 0

        @pl.when(by_hop)
        def _():
            to_hop(core).start()

        @pl.when(jnp.logical_not(by_hop))
        def _():
            partial_out(0, core, across).start()

    rhs = gather(order[1])
    for core in range(2):
        part[core] = product(core, rhs)

        @pl.when(joins if core in HOPS else c < 0)
        def _():
            with jax.named_scope("hop"):
                arrived(hop.at[core], hop_r.at[core])
            part[core] = part[core] + decode(hop[core])

        @pl.when(beside != c)
        def _():
            out_buf[1, core] = encode(part[core])
            partial_out(1, core, beside).start()

    @pl.when(beside == c)
    def _():
        to_near().start()

    @pl.when(keeper != e)
    def _():
        with jax.named_scope("near"):
            arrived(near.at[0], near_r.at[0])

    @pl.when(keeper == e)
    def _():
        near[0] = part[e]

    load_prune.wait()
    for k in range(1, C):
        s = flip(c, k)

        def take():
            with jax.named_scope("partial"):
                arrived(in_buf.at[s], zr.at[s])
            near[0] = near[0] + decode(in_buf[s])

        if k == C - 1:
            pl.when(jnp.logical_or(c != C - 1, e != HOPS[0]))(take)
        else:
            take()

    own = near[0]
    kept = own * prune_buf[...].astype(jnp.float32)
    inflated = kept * kept
    infl_out[...] = inflated
    tots[r] = jnp.broadcast_to(
        jnp.sum(inflated, axis=0, keepdims=True), tots.shape[1:]
    )
    for k in range(1, R):
        there = flip(r, R - k)
        remote(
            tots.at[r], tots.at[r], ts.at[0], tr.at[0], lax.div(there, 2), lax.rem(there, 2), c
        ).start()
    peers = tots.at[pl.ds(0, R - 1)]
    with jax.named_scope("totals"):
        arrived(peers, tr.at[0])
    total = tots[0]
    for k in range(1, R):
        total = total + tots[k]
    tot_out[...] = total / (rows * R) + 1e-05

    with jax.named_scope("sent"):
        for copy in sends:
            copy.wait_send()
        passed = bk.at[:, :, pl.ds(0, C - 1)]
        remote(passed, passed, s2.at[0], r2.at[0], p, e, c).wait_send()
        remote(peers, peers, ts.at[0], tr.at[0], p, e, c).wait_send()
        for q in range(C):
            @pl.when(jnp.logical_not(stays(q)))
            def _():
                scatter(q).wait_send()
        for core in range(2):
            by_hop = lends if core in HOPS else c < 0

            @pl.when(by_hop)
            def _():
                to_hop(core).wait_send()

            @pl.when(jnp.logical_not(by_hop))
            def _():
                partial_out(0, core, across).wait_send()

            @pl.when(beside != c)
            def _():
                partial_out(1, core, beside).wait_send()

        @pl.when(beside == c)
        def _():
            to_near().wait_send()


def kernel_body(R, C, matrix, occ_matrix, batch, occ_batch, prune_mask):
    rows, depth = matrix.shape
    cols = batch.shape[1]
    half = C // 2
    vmem, hbm = (pl.BlockSpec(memory_space=s) for s in (pltpu.VMEM, pltpu.HBM))
    dma = pltpu.SemaphoreType.DMA
    f32, bf16 = jnp.float32, jnp.bfloat16
    inflated, total = pl.pallas_call(
        functools.partial(kernel, R, C),
        out_shape=(
            pltpu.VMEM((rows, cols), f32),
            pltpu.VMEM((1, cols), f32),
        ),
        in_specs=[hbm] * 5,
        out_specs=(vmem, vmem),
        scratch_shapes=[
            pltpu.VMEM((2, rows, depth), bf16),
            pltpu.SMEM(occ_matrix.shape, jnp.int32),
            pltpu.VMEM((rows, cols), bf16),
            pltpu.SMEM(occ_batch.shape[:1], jnp.int32),
            pltpu.VMEM((rows, cols), jnp.int32),
            pltpu.VMEM((rows, cols), bf16),
            pltpu.VMEM((half, 2, C, rows // C, cols), bf16),
            pltpu.VMEM((2, rows, cols), f32),
            pltpu.VMEM((1, rows, cols), f32),
            pltpu.VMEM((half, 2, rows, cols), jnp.int16),
            pltpu.VMEM((C, rows, cols), jnp.int16),
            pltpu.VMEM((2, rows, cols), jnp.int16),
            pltpu.VMEM((R, 1, cols), f32),
            dma((5,)),
            dma((1,)),
            dma((1,)),
            dma((C,)),
            dma((half, 2)),
            dma((1,)),
            dma((half,)),
            dma((half, 2)),
            dma((C,)),
            dma((1,)),
            dma((1,)),
            dma((1,)),
            dma((1,)),
            dma((2,)),
            dma((2,)),
            pltpu.SemaphoreType.REGULAR((half, 2)),
            pltpu.SemaphoreType.REGULAR((1,)),
        ],
        compiler_params=pltpu.CompilerParams(
            collective_id=0, has_side_effects=True, vmem_limit_bytes=32 * 2**20
        ),
    )(*(
        pltpu.with_memory_space_constraint(x, pltpu.HBM)
        for x in (matrix, occ_matrix, batch, occ_batch[:, 0], prune_mask)
    ))
    return inflated / total


def body(R, C, matrix, occ_matrix, batch, occ_batch, prune_mask):
    rows = matrix.shape[0]
    fits = (
        C == 4 and R == 2 * C
        and rows % (16 * C) == 0 and matrix.shape[1] == rows * 2
    )
    chosen = functools.partial(kernel_body, R, C) if fits else plain_body
    return chosen(matrix, occ_matrix, batch, occ_batch, prune_mask)


def solution(mesh):
    R, C = mesh.shape["row"], mesh.shape["col"]
    placed = (P("row", "col"),) * 5
    return jax.shard_map(
        functools.partial(body, R, C), mesh=mesh, in_specs=placed,
        out_specs=P("row", "col"), check_vma=False,
    )
```

```python
import functools

import jax
import jax.numpy as jnp
from jax import lax
from jax.experimental import pallas as pl
from jax.experimental.pallas import tpu as pltpu
from jax.sharding import PartitionSpec as P

MESH = pl.DeviceIdType.MESH

LOWEST = -20.5
STEPS = 2730.0
HOPS = (1,)
LN2 = 0.6931471805599453


def encode(x):
    safe = jnp.maximum(x, 2.0**LOWEST)
    level = jnp.minimum((jnp.log(safe) * (1.0 / LN2) - LOWEST) * STEPS, 65533.0) + 1.5
    code = jnp.where(x > 0, level.astype(jnp.int32), 0)
    return (code - 32768).astype(jnp.int16)


def decode(code):
    level = code.astype(jnp.int32) + 32767
    value = jnp.exp((level.astype(jnp.float32) * (1.0 / STEPS) + LOWEST) * LN2)
    return jnp.where(level >= 0, value, 0.0)


def expand_tiles(occupancy, size):
    return jnp.repeat(jnp.repeat(occupancy, size, axis=0), size, axis=1)


def plain_body(matrix, occ_matrix, batch, occ_batch, prune_mask):
    tile_size = matrix.shape[0] // occ_matrix.shape[0]
    stored_matrix = matrix * expand_tiles(occ_matrix, tile_size).astype(jnp.bfloat16)
    stored_batch = batch * expand_tiles(occ_batch, tile_size).astype(jnp.bfloat16)
    whole_batch = lax.all_gather(stored_batch, "row", axis=0, tiled=True)
    expanded = jnp.dot(
        lax.all_gather(stored_matrix, "col", axis=1, tiled=True),
        whole_batch,
        preferred_element_type=jnp.float32,
    )
    kept = expanded * prune_mask.astype(jnp.float32)
    inflated = kept * kept
    col_total = lax.psum(jnp.sum(inflated, axis=0), "row")
    order = matrix.shape[0] * lax.axis_size("row")
    return inflated / (col_total[None, :] / order + 1e-05)


def kernel(
    R, C, mat_hbm, occ_m_hbm, bat_hbm, occ_b_hbm, prune_hbm, infl_out, tot_out,
    both, occ_m, bat, occ_b, prune_buf, sb, bk, part, near, out_buf, in_buf, hop, tots,
    load_sems, swap_s, swap_r, s1, r1, s2, r2, zs, zr, near_r, ts, tr,
    hop_r, ready, ready_row,
):
    half = C // 2
    _, rows, depth = both.shape
    piece = rows // C
    tile = rows // occ_m_hbm.shape[0]
    r, c = lax.axis_index("row"), lax.axis_index("col")
    p, e = lax.div(r, 2), lax.rem(r, 2)
    other = 1 - e
    keeper, slot = 1 - lax.div(c, half), lax.rem(c, half)
    mine_half = 1 - e

    def flip(at, k):
        for bit in (1, 2, 4):
            if k & bit:
                at = at + bit * (1 - 2 * lax.rem(lax.div(at, bit), 2))
        return at

    def remote(src, dst, ssem, rsem, chip, core, plane):
        return pltpu.make_async_remote_copy(
            src_ref=src, dst_ref=dst, send_sem=ssem, recv_sem=rsem,
            device_id={"row": chip * 2 + core, "col": plane}, device_id_type=MESH,
        )

    def arrived(ref, rsem):
        remote(ref, ref, s1.at[0], rsem, p, e, c).wait_recv()

    def signal(sem, chip, core, plane):
        pl.semaphore_signal(
            sem, inc=1, device_id={"row": chip * 2 + core, "col": plane},
            device_id_type=MESH,
        )

    barrier = pltpu.get_barrier_semaphore()

    def guarded(condition, *args):
        @pl.when(condition)
        def _():
            signal(*args)

    for n in range(half):
        b = mine_half * half + n
        for core in range(2):
            guarded(b != c, barrier, c, core, b)
    crossing = keeper != e
    lends = jnp.logical_and(crossing, c == 0)
    joins = jnp.logical_and(crossing, c == 1)
    guarded(joins, barrier, p, e, 0)
    for k in range(R):
        guarded(k > r, barrier, k // 2, k % 2, c)
    for n in range(half):
        b = mine_half * half + n
        for core in range(2):
            guarded(b > c, barrier, p, core, b)
    for s in range(1, C):
        guarded(s > c, barrier, p, keeper, s)

    def load(n, src, dst):
        copy = pltpu.make_async_copy(src, dst, load_sems.at[n])
        copy.start()
        return copy

    load_b = load(0, bat_hbm, bat)
    load_ob = load(1, occ_b_hbm, occ_b)
    load_a = load(2, mat_hbm, both.at[e])
    load_om = load(3, occ_m_hbm, occ_m)
    load_prune = load(4, prune_hbm, prune_buf)
    load_ob.wait()
    load_b.wait()
    for t in range(rows // tile):
        at = pl.ds(t * tile, tile)
        sb[at, :] = bat[at, :] * occ_b[t].astype(jnp.float32).astype(jnp.bfloat16)

    earlier = r + c + jnp.where(p != c, C, 0) + jnp.where(lends, 1, 0)
    for n in range(half):
        earlier = earlier + jnp.where(mine_half * half + n < c, 2, 0)
    with jax.named_scope("greeted"):
        pl.semaphore_wait(barrier, earlier)

    def scatter(q):
        return remote(
            sb.at[pl.ds(q * piece, piece)], bk.at[slot, e, q],
            s1.at[0], r1.at[slot, e], q, keeper, p,
        )

    def stays(q):
        return jnp.logical_and(jnp.logical_and(p == q, c == p), keeper == e)

    def spread():
        for k in range(C - 1, -1, -1):
            q = flip(p, k)

            @pl.when(stays(q))
            def _():
                pltpu.make_async_copy(
                    sb.at[pl.ds(q * piece, piece)], bk.at[slot, e, q], r1.at[slot, e]
                ).start()

            @pl.when(jnp.logical_not(stays(q)))
            def _():
                scatter(q).start()

    crosses = lax.div(p, half) != lax.div(c, half)
    pl.when(p != c)(spread)
    for k in range(R):
        guarded(k < r, ready_row.at[0], k // 2, k % 2, c)
    for s in range(C - 1):
        guarded(s < c, ready.at[0], p, keeper, s)

    load_om.wait()
    load_a.wait()
    for i in range(rows // tile):
        for j in range(depth // tile):
            at = (e, pl.ds(i * tile, tile), pl.ds(j * tile, tile))
            both[at] = both[at] * occ_m[i, j].astype(jnp.float32).astype(jnp.bfloat16)

    @pl.when(r < R - 1)
    def _():
        with jax.named_scope("row"):
            pl.semaphore_wait(ready_row.at[0], R - 1 - r)

    sends = []

    def send(*args):
        copy = remote(*args)
        copy.start()
        sends.append(copy)

    send(both.at[e], both.at[e], swap_s.at[0], swap_r.at[0], p, other, c)
    pl.when(p == c)(spread)

    first = jnp.where(keeper == e, 1 - slot, jnp.where(c == 1, 0, mine_half))
    order = [first, 1 - first]

    def pass_on(n, at):
        for core in range(2):
            mine = bk.at[at, core, p]
            with jax.named_scope("piece"):
                arrived(mine, r1.at[at, core])
            for k in range(C - 1, 0, -1):
                remote(mine, mine, s2.at[0], r2.at[at], flip(p, k), e, c).start()

    def gather(at):
        with jax.named_scope("block"):
            arrived(bk.at[at, :, pl.ds(0, C - 1)], r2.at[at])
        return bk[at].reshape(depth, bk.shape[-1])

    def product(core, rhs):
        return jnp.dot(both[core], rhs, preferred_element_type=jnp.float32)

    def partial_out(n, core, b):
        return remote(out_buf.at[n, core], in_buf.at[c], zs.at[n], zr.at[c], p, core, b)

    def to_hop(core):
        return remote(out_buf.at[0, core], hop.at[0], zs.at[0], hop_r.at[0], p, e, 1)

    def to_near():
        return remote(part.at[other], near.at[0], zs.at[1], near_r.at[0], p, other, c)

    across, beside = mine_half * half + order[0], mine_half * half + order[1]
    pass_on(0, order[0])
    with jax.named_scope("swap"):
        arrived(both.at[other], swap_r.at[0])
    pass_on(1, order[1])
    rhs = gather(order[0])
    later = jnp.int32(0)
    for n in range(half):
        later = later + jnp.where(mine_half * half + n > c, 2, 0)

    @pl.when(later > 0)
    def _():
        pl.semaphore_wait(ready.at[0], later)

    for core in range(2):
        part[core] = product(core, rhs)

        out_buf[0, core] = encode(part[core])


        by_hop = lends if core in HOPS else c < 0

        @pl.when(by_hop)
        def _():
            to_hop(core).start()

        @pl.when(jnp.logical_not(by_hop))
        def _():
            partial_out(0, core, across).start()

    rhs = gather(order[1])
    for core in range(2):
        part[core] = product(core, rhs)

        @pl.when(joins if core in HOPS else c < 0)
        def _():
            with jax.named_scope("hop"):
                arrived(hop.at[0], hop_r.at[0])
            part[core] = part[core] + decode(hop[0])

        @pl.when(beside != c)
        def _():
            out_buf[1, core] = encode(part[core])
            partial_out(1, core, beside).start()

    @pl.when(beside == c)
    def _():
        to_near().start()

    @pl.when(keeper != e)
    def _():
        with jax.named_scope("near"):
            arrived(near.at[0], near_r.at[0])

    @pl.when(keeper == e)
    def _():
        near[0] = part[e]

    load_prune.wait()
    for k in range(1, C):
        s = flip(c, k)

        def take():
            with jax.named_scope("partial"):
                arrived(in_buf.at[s], zr.at[s])
            near[0] = near[0] + decode(in_buf[s])

        if k == C - 1:
            pl.when(jnp.logical_or(c != C - 1, e != HOPS[0]))(take)
        else:
            take()

    own = near[0]
    kept = own * prune_buf[...].astype(jnp.float32)
    inflated = kept * kept
    infl_out[...] = inflated
    tots[r] = jnp.broadcast_to(
        jnp.sum(inflated, axis=0, keepdims=True), tots.shape[1:]
    )
    for k in range(1, R):
        there = flip(r, R - k)
        remote(
            tots.at[r], tots.at[r], ts.at[0], tr.at[0], lax.div(there, 2), lax.rem(there, 2), c
        ).start()
    peers = tots.at[pl.ds(0, R - 1)]
    with jax.named_scope("totals"):
        arrived(peers, tr.at[0])
    total = tots[0]
    for k in range(1, R):
        total = total + tots[k]
    tot_out[...] = total / (rows * R) + 1e-05

    with jax.named_scope("sent"):
        for copy in sends:
            copy.wait_send()
        passed = bk.at[:, :, pl.ds(0, C - 1)]
        remote(passed, passed, s2.at[0], r2.at[0], p, e, c).wait_send()
        remote(peers, peers, ts.at[0], tr.at[0], p, e, c).wait_send()
        for whole, count in ((True, C), (False, C - 1)):
            @pl.when(stays(p) != whole)
            def _():
                spread_out = sb.at[pl.ds(0, count * piece)]
                remote(spread_out, spread_out, s1.at[0], r1.at[0, 0], p, e, c).wait_send()

        remote(out_buf.at[0], out_buf.at[0], zs.at[0], zr.at[0], p, e, c).wait_send()

        @pl.when(beside != c)
        def _():
            remote(out_buf.at[1], out_buf.at[1], zs.at[1], zr.at[0], p, e, c).wait_send()

        @pl.when(beside == c)
        def _():
            to_near().wait_send()


def kernel_body(R, C, matrix, occ_matrix, batch, occ_batch, prune_mask):
    rows, depth = matrix.shape
    cols = batch.shape[1]
    half = C // 2
    vmem, hbm = (pl.BlockSpec(memory_space=s) for s in (pltpu.VMEM, pltpu.HBM))
    dma = pltpu.SemaphoreType.DMA
    f32, bf16 = jnp.float32, jnp.bfloat16
    inflated, total = pl.pallas_call(
        functools.partial(kernel, R, C),
        out_shape=(
            pltpu.VMEM((rows, cols), f32),
            pltpu.VMEM((1, cols), f32),
        ),
        in_specs=[hbm] * 5,
        out_specs=(vmem, vmem),
        scratch_shapes=[
            pltpu.VMEM((2, rows, depth), bf16),
            pltpu.SMEM(occ_matrix.shape, jnp.int32),
            pltpu.VMEM((rows, cols), bf16),
            pltpu.SMEM(occ_batch.shape[:1], jnp.int32),
            pltpu.VMEM((rows, cols), jnp.int32),
            pltpu.VMEM((rows, cols), bf16),
            pltpu.VMEM((half, 2, C, rows // C, cols), bf16),
            pltpu.VMEM((2, rows, cols), f32),
            pltpu.VMEM((1, rows, cols), f32),
            pltpu.VMEM((half, 2, rows, cols), jnp.int16),
            pltpu.VMEM((C, rows, cols), jnp.int16),
            pltpu.VMEM((1, rows, cols), jnp.int16),
            pltpu.VMEM((R, 1, cols), f32),
            dma((5,)),
            dma((1,)),
            dma((1,)),
            dma((1,)),
            dma((half, 2)),
            dma((1,)),
            dma((half,)),
            dma((half,)),
            dma((C,)),
            dma((1,)),
            dma((1,)),
            dma((1,)),
            dma((1,)),
            pltpu.SemaphoreType.REGULAR((1,)),
            pltpu.SemaphoreType.REGULAR((1,)),
        ],
        compiler_params=pltpu.CompilerParams(
            collective_id=0, has_side_effects=True, vmem_limit_bytes=32 * 2**20
        ),
    )(*(
        pltpu.with_memory_space_constraint(x, pltpu.HBM)
        for x in (matrix, occ_matrix, batch, occ_batch[:, 0], prune_mask)
    ))
    return inflated / total


def body(R, C, matrix, occ_matrix, batch, occ_batch, prune_mask):
    rows = matrix.shape[0]
    fits = (
        C == 4 and R == 2 * C
        and rows % (16 * C) == 0 and matrix.shape[1] == rows * 2
    )
    chosen = functools.partial(kernel_body, R, C) if fits else plain_body
    return chosen(matrix, occ_matrix, batch, occ_batch, prune_mask)


def solution(mesh):
    R, C = mesh.shape["row"], mesh.shape["col"]
    placed = (P("row", "col"),) * 5
    return jax.shard_map(
        functools.partial(body, R, C), mesh=mesh, in_specs=placed,
        out_specs=P("row", "col"), check_vma=False,
    )
```
